256 devices in a mesh: gx: 8 (over y, core), gy: 4 (over x), gz: 8 (over z).
Axes of the slice: x: 4, y: 4, z: 8, core: 2. Of those that a mesh axis runs over, the one named last changes fastest.
Arguments:
- rhs: float32 [4, 64, 256, 1024], P(None, 'gz', 'gx', 'gy'), may hold values from -6 to 6
- coef_x: float32 [64, 256, 1024], P('gz', 'gx', 'gy'), may hold values from 0.3 to 3
- coef_y: float32 [64, 256, 1024], P('gz', 'gx', 'gy'), may hold values from 0.3 to 3
- coef_z: float32 [64, 256, 1024], P('gz', 'gx', 'gy'), may hold values from 0.3 to 3
- diag_term: float32 [64, 256, 1024], P('gz', 'gx', 'gy'), may hold values from 0.2 to 2
Outputs:
- ortho_basis: float32 [20, 64, 256, 1024], P(None, 'gz', 'gx', 'gy')
- triangle: float32 [20, 20], replicated
The draws below stay inside these ranges and needn't reach their ends.
All inputs are finite; a program needn't handle non-finite values.
Results may differ from the reference program's by a relative error of at most 0.0003.
Values sent between devices are 32-bit elements; how exact they have to be, the bound alone decides.
A program may use at most 128 MiB of HBM per device.

```python
import math
import jax
import jax.numpy as jnp
from jax import lax

NRHS = 4
STEPS = 4
COLS = 20
NX = 256
NY = 1024
NZ = 64


def draw_rhs(key, part):
    common_key = jax.random.fold_in(key, 11)
    own_key = jax.random.fold_in(key, 12)
    common = jnp.clip(jax.random.normal(common_key, (1, NZ, NX, NY), jnp.float32), -6.0, 6.0)
    own = jnp.clip(jax.random.normal(own_key, (NRHS, NZ, NX, NY), jnp.float32), -6.0, 6.0)
    return jnp.clip(0.9 * common + 0.1 * own, -6.0, 6.0)


def shard_levels(key, dims, split, smallest, top_value):
    level = 1.0
    for position, blocks in split:
        heights = jax.random.uniform(jax.random.fold_in(jax.random.fold_in(key, 6), position), (blocks,), jnp.float32, smallest / len(split), top_value / len(split))
        level = level * jnp.repeat(jnp.exp(heights), dims[position] // blocks).reshape((-1,) + (1,) * (len(dims) - 1 - position))
    return level


def setup_inputs(seed: int = 0) -> dict:
    arg_keys = jax.random.split(jax.random.key(seed), 6)
    return {
        "rhs": draw_rhs(jax.random.fold_in(arg_keys[5], 71), 0),
        "coef_x": jnp.clip(jnp.exp(math.log(3.0) - 2.3025851 * jax.random.uniform(arg_keys[1], (NZ, NX, NY), jnp.float32) ** shard_levels(arg_keys[1], (NZ, NX, NY), ((0, 8), (1, 8), (2, 4)), -0.2, 0.2)), 0.3, 3.0),
        "coef_y": jnp.clip(jnp.exp(math.log(3.0) - 2.3025851 * jax.random.uniform(arg_keys[2], (NZ, NX, NY), jnp.float32) ** shard_levels(arg_keys[2], (NZ, NX, NY), ((0, 8), (1, 8), (2, 4)), -0.2, 0.2)), 0.3, 3.0),
        "coef_z": jnp.clip(jnp.exp(math.log(3.0) - 2.3025851 * jax.random.uniform(arg_keys[3], (NZ, NX, NY), jnp.float32) ** shard_levels(arg_keys[3], (NZ, NX, NY), ((0, 8), (1, 8), (2, 4)), -0.2, 0.2)), 0.3, 3.0),
        "diag_term": jnp.clip(0.2 + 1.8 * jax.random.uniform(arg_keys[4], (NZ, NX, NY), jnp.float32) ** shard_levels(arg_keys[4], (NZ, NX, NY), ((0, 8), (1, 8), (2, 4)), -0.2, 0.2), 0.2, 2.0),
    }


NEWTON_SHIFTS = (3.0, 11.0, 7.0, 1.5)
BASIS_SCALE = 1.0 / 6.0

def inner_part(array, off_z, off_x, off_y, margin=1):
    size_z, size_x, size_y = array.shape[-3:]
    return array[..., margin + off_z:size_z - margin + off_z, margin + off_x:size_x - margin + off_x, margin + off_y:size_y - margin + off_y]

def face_term(field, center, coef, off_z, off_x, off_y):
    upper = 0.5 * (inner_part(coef, 0, 0, 0) + inner_part(coef, off_z, off_x, off_y))
    lower = 0.5 * (inner_part(coef, 0, 0, 0) + inner_part(coef, -off_z, -off_x, -off_y))
    return upper * (center - inner_part(field, off_z, off_x, off_y)) + lower * (center - inner_part(field, -off_z, -off_x, -off_y))

def apply_operator(field, coef_z, coef_x, coef_y, diag_pad):
    center = inner_part(field, 0, 0, 0)
    image = inner_part(diag_pad, 0, 0, 0) * center
    image = image + face_term(field, center, coef_z, 1, 0, 0)
    image = image + face_term(field, center, coef_x, 0, 1, 0)
    image = image + face_term(field, center, coef_y, 0, 0, 1)
    return image

def pad_cells(array):
    widths = [(0, 0)] * (array.ndim - 3) + [(1, 1)] * 3
    return jnp.pad(array, widths)

def upper_cholesky(gram):
    order = gram.shape[0]
    column_ids = jnp.arange(order, dtype=jnp.int32)
    factor_rows = []
    for row_id in range(order):
        accum = gram[row_id]
        if factor_rows:
            earlier = jnp.stack(factor_rows, 0)
            accum = accum - lax.optimization_barrier(jnp.sum(earlier[:, row_id:row_id + 1] * earlier, 0))
        pivot = jnp.sqrt(accum[row_id])
        factor_rows.append(jnp.where(column_ids >= row_id, accum / pivot, jnp.zeros_like(accum)))
    return jnp.stack(factor_rows, 0)

def upper_inverse(factor):
    order = factor.shape[0]
    identity_mat = jnp.eye(order, dtype=factor.dtype)
    solved = [None] * order
    for row_id in range(order - 1, -1, -1):
        accum = identity_mat[row_id]
        if row_id < order - 1:
            later = jnp.stack(solved[row_id + 1:], 0)
            accum = accum - lax.optimization_barrier(jnp.sum(factor[row_id, row_id + 1:][:, None] * later, 0))
        solved[row_id] = accum / factor[row_id, row_id]
    return jnp.stack(solved, 0)

def orthonormalize(rows, count):
    gram = jnp.dot(rows, rows.T, precision=lax.Precision.HIGHEST)
    factor = upper_cholesky(gram / count)
    inverse = upper_inverse(factor)
    return (jnp.dot(inverse.T, rows, precision=lax.Precision.HIGHEST), factor)

def reference(rhs, coef_x, coef_y, coef_z, diag_term):
    pad_z = pad_cells(coef_z)
    pad_x = pad_cells(coef_x)
    pad_y = pad_cells(coef_y)
    pad_diag = pad_cells(diag_term)
    field = rhs
    blocks = [rhs]
    for section in range(STEPS):
        image = apply_operator(pad_cells(field), pad_z, pad_x, pad_y, pad_diag)
        field = (image - NEWTON_SHIFTS[section] * field) * BASIS_SCALE
        blocks.append(field)
    basis = jnp.concatenate(blocks, 0)
    count = float(NZ * NX * NY)
    rows = basis.reshape(COLS, -1)
    first, factor_one = orthonormalize(rows, count)
    second, factor_two = orthonormalize(first, count)
    return (second.reshape(basis.shape), jnp.dot(factor_two, factor_one, precision=lax.Precision.HIGHEST))
```

```python
import jax
import jax.numpy as jnp
from jax import lax
from jax.experimental import pallas as pl
from jax.sharding import PartitionSpec as P

STEPS = 4


NEWTON_SHIFTS = (3.0, 11.0, 7.0, 1.5)
BASIS_SCALE = 1.0 / 6.0
AXES = ("gx", "gy", "gz")


def neighbours(value, axis_name, dim):
    count = lax.axis_size(axis_name)
    length = value.shape[dim]
    up = [(i, i + 1) for i in range(count - 1)]
    down = [(i + 1, i) for i in range(count - 1)]
    last = lax.slice_in_dim(value, length - 1, length, axis=dim)
    first = lax.slice_in_dim(value, 0, 1, axis=dim)
    below = lax.ppermute(last, axis_name, up)
    above = lax.ppermute(first, axis_name, down)
    return below, above


def shifted(value, dim, below, above):
    length = value.shape[dim]
    minus = jnp.concatenate([below, lax.slice_in_dim(value, 0, length - 1, axis=dim)], axis=dim)
    plus = jnp.concatenate([lax.slice_in_dim(value, 1, length, axis=dim), above], axis=dim)
    return minus, plus


def face_coefs(coef, axis_name, dim):
    below, above = neighbours(coef, axis_name, dim)
    minus, plus = shifted(coef, dim, below, above)
    return 0.5 * (coef + plus), 0.5 * (coef + minus)


def chol_kernel(g_ref, r_ref, x_ref):
    n = g_ref.shape[0]
    a = g_ref[...]
    rows = lax.broadcasted_iota(jnp.int32, (n, n), 0)
    cols = lax.broadcasted_iota(jnp.int32, (n, n), 1)
    lane = cols[0:1, :]
    sub = rows[:, 0:1]
    r = jnp.zeros((n, n), jnp.float32)
    rt = jnp.zeros((n, n), jnp.float32)
    pivots = []
    for k in range(n):
        rowk = jnp.sum(jnp.where(rows == k, a, 0.0), axis=0, keepdims=True)
        colk = jnp.sum(jnp.where(cols == k, a, 0.0), axis=1, keepdims=True)
        piv = jnp.sqrt(jnp.sum(jnp.where(lane == k, rowk, 0.0), axis=1, keepdims=True))
        rrow = jnp.where(lane >= k, rowk / piv, 0.0)
        rcol = jnp.where(sub >= k, colk / piv, 0.0)
        r = jnp.where(rows == k, rrow, r)
        rt = jnp.where(cols == k, rcol, rt)
        a = a - rcol * rrow
        pivots.append(piv)
    x = jnp.zeros((n, n), jnp.float32)
    for i in range(n - 1, -1, -1):
        ident = jnp.where(lane == i, 1.0, 0.0)
        if i < n - 1:
            c = jnp.sum(jnp.where(cols == i, rt, 0.0), axis=1, keepdims=True)
            s = jnp.sum(jnp.where(sub > i, c * x, 0.0), axis=0, keepdims=True)
            ident = ident - s
        x = jnp.where(rows == i, ident / pivots[i], x)
    r_ref[...] = r
    x_ref[...] = x


def factor_and_inverse(gram):
    n = gram.shape[0]
    return pl.pallas_call(
        chol_kernel,
        out_shape=(
            jax.ShapeDtypeStruct((n, n), jnp.float32),
            jax.ShapeDtypeStruct((n, n), jnp.float32),
        ),
    )(gram)


def total_gram(rows):
    gram = jnp.dot(rows, rows.T, precision=lax.Precision.HIGHEST)
    for axis in AXES:
        gram = lax.psum(gram, axis)
    return gram


def orthonormalize(rows, count):
    gram = total_gram(rows)
    factor, inverse = factor_and_inverse(gram / count)
    return (jnp.dot(inverse.T, rows, precision=lax.Precision.HIGHEST), factor)


def body(rhs, coef_x, coef_y, coef_z, diag_term):
    up_z, lo_z = face_coefs(coef_z, "gz", 0)
    up_x, lo_x = face_coefs(coef_x, "gx", 1)
    up_y, lo_y = face_coefs(coef_y, "gy", 2)
    blocks = [rhs]
    field = rhs
    for section in range(STEPS):
        bz, az = neighbours(field, "gz", 1)
        bx, ax = neighbours(field, "gx", 2)
        by, ay = neighbours(field, "gy", 3)
        mz, pz = shifted(field, 1, bz, az)
        mx, px = shifted(field, 2, bx, ax)
        my, py = shifted(field, 3, by, ay)
        center = field
        image = diag_term * center
        image = image + (up_z * (center - pz) + lo_z * (center - mz))
        image = image + (up_x * (center - px) + lo_x * (center - mx))
        image = image + (up_y * (center - py) + lo_y * (center - my))
        field = (image - NEWTON_SHIFTS[section] * field) * BASIS_SCALE
        blocks.append(field)
    basis = jnp.concatenate(blocks, 0)
    rows = basis.reshape(basis.shape[0], -1)
    count = float(rows.shape[1] * lax.axis_size("gx") * lax.axis_size("gy") * lax.axis_size("gz"))
    first, factor_one = orthonormalize(rows, count)
    second, factor_two = orthonormalize(first, count)
    return (
        second.reshape(basis.shape),
        jnp.dot(factor_two, factor_one, precision=lax.Precision.HIGHEST),
    )


def solution(mesh):
    return jax.shard_map(
        body,
        mesh=mesh,
        in_specs=(
            P(None, "gz", "gx", "gy"),
            P("gz", "gx", "gy"),
            P("gz", "gx", "gy"),
            P("gz", "gx", "gy"),
            P("gz", "gx", "gy"),
        ),
        out_specs=(P(None, "gz", "gx", "gy"), P()),
        check_vma=False,
    )
```

```python
import jax
import jax.numpy as jnp
from jax import lax
import functools
from jax.experimental import pallas as pl
from jax.experimental.pallas import tpu as pltpu
from jax.sharding import PartitionSpec as P

STEPS = 4


NEWTON_SHIFTS = (3.0, 11.0, 7.0, 1.5)
BASIS_SCALE = 1.0 / 6.0
AXES = ("gx", "gy", "gz")


def neighbours(value, axis_name, dim):
    count = lax.axis_size(axis_name)
    length = value.shape[dim]
    up = [(i, i + 1) for i in range(count - 1)]
    down = [(i + 1, i) for i in range(count - 1)]
    last = lax.slice_in_dim(value, length - 1, length, axis=dim)
    first = lax.slice_in_dim(value, 0, 1, axis=dim)
    below = lax.ppermute(last, axis_name, up)
    above = lax.ppermute(first, axis_name, down)
    return below, above


def shifted(value, dim, below, above):
    length = value.shape[dim]
    minus = jnp.concatenate([below, lax.slice_in_dim(value, 0, length - 1, axis=dim)], axis=dim)
    plus = jnp.concatenate([lax.slice_in_dim(value, 1, length, axis=dim), above], axis=dim)
    return minus, plus


def face_coefs(coef, axis_name, dim):
    below, above = neighbours(coef, axis_name, dim)
    minus, plus = shifted(coef, dim, below, above)
    return 0.5 * (coef + plus), 0.5 * (coef + minus)


def cholesky_and_inverse(a, r_ref, x_ref):
    n = a.shape[0]
    rows = lax.broadcasted_iota(jnp.int32, (n, n), 0)
    cols = lax.broadcasted_iota(jnp.int32, (n, n), 1)
    lane = cols[0:1, :]
    sub = rows[:, 0:1]
    r = jnp.zeros((n, n), jnp.float32)
    rt = jnp.zeros((n, n), jnp.float32)
    pivots = []
    for k in range(n):
        rowk = jnp.sum(jnp.where(rows == k, a, 0.0), axis=0, keepdims=True)
        colk = jnp.sum(jnp.where(cols == k, a, 0.0), axis=1, keepdims=True)
        piv = jnp.sqrt(jnp.sum(jnp.where(lane == k, rowk, 0.0), axis=1, keepdims=True))
        rrow = jnp.where(lane >= k, rowk / piv, 0.0)
        rcol = jnp.where(sub >= k, colk / piv, 0.0)
        r = jnp.where(rows == k, rrow, r)
        rt = jnp.where(cols == k, rcol, rt)
        a = a - rcol * rrow
        pivots.append(piv)
    x = jnp.zeros((n, n), jnp.float32)
    for i in range(n - 1, -1, -1):
        ident = jnp.where(lane == i, 1.0, 0.0)
        if i < n - 1:
            c = jnp.sum(jnp.where(cols == i, rt, 0.0), axis=1, keepdims=True)
            s = jnp.sum(jnp.where(sub > i, c * x, 0.0), axis=0, keepdims=True)
            ident = ident - s
        x = jnp.where(rows == i, ident / pivots[i], x)
    r_ref[...] = r
    x_ref[...] = x


def gram_kernel(sizes, count, g_ref, r_ref, x_ref, bx, by, bz, s1, s2, send_sem, recv_sem):
    bufs = (bx, by, bz)
    me = tuple(lax.axis_index(a) for a in AXES)

    def device(axis, index):
        return tuple(index if j == axis else me[j] for j in range(3))

    for buf in bufs:
        buf[...] = jnp.zeros_like(buf)
    barrier = pltpu.get_barrier_semaphore()
    peers = 0
    for axis in range(3):
        n = sizes[axis]
        for d in range(1, n):
            pl.semaphore_signal(barrier, inc=1, device_id=device(axis, (me[axis] + d) % n), device_id_type=pl.DeviceIdType.MESH)
            peers += 1
    pl.semaphore_wait(barrier, peers)

    src = g_ref
    total = None
    for axis, dst in zip(range(3), (s1, s2, None)):
        n = sizes[axis]
        m = me[axis]
        buf = bufs[axis]
        sends = []
        for d in range(1, n):
            copy = pltpu.make_async_remote_copy(
                src_ref=src,
                dst_ref=buf.at[m],
                send_sem=send_sem.at[axis, d],
                recv_sem=recv_sem.at[axis, m],
                device_id=device(axis, (m + d) % n),
                device_id_type=pl.DeviceIdType.MESH,
            )
            copy.start()
            sends.append(copy)
        for d in range(1, n):
            q = (m + n - d) % n
            pltpu.make_async_remote_copy(
                src_ref=src,
                dst_ref=buf.at[q],
                send_sem=send_sem.at[axis, d],
                recv_sem=recv_sem.at[axis, q],
                device_id=device(axis, q),
                device_id_type=pl.DeviceIdType.MESH,
            ).wait_recv()
        own = src[...]
        total = None
        for slot in range(n):
            value = jnp.where(m == slot, own, buf[slot])
            total = value if total is None else total + value
        for copy in sends:
            copy.wait_send()
        if dst is not None:
            dst[...] = total
            src = dst
    cholesky_and_inverse(total / count, r_ref, x_ref)


def factor_and_inverse(partial, count):
    n = partial.shape[0]
    sizes = tuple(lax.axis_size(a) for a in AXES)
    most = max(sizes)
    return pl.pallas_call(
        functools.partial(gram_kernel, sizes, count),
        out_shape=(
            jax.ShapeDtypeStruct((n, n), jnp.float32),
            jax.ShapeDtypeStruct((n, n), jnp.float32),
        ),
        scratch_shapes=[
            pltpu.VMEM((sizes[0], n, n), jnp.float32),
            pltpu.VMEM((sizes[1], n, n), jnp.float32),
            pltpu.VMEM((sizes[2], n, n), jnp.float32),
            pltpu.VMEM((n, n), jnp.float32),
            pltpu.VMEM((n, n), jnp.float32),
            pltpu.SemaphoreType.DMA((3, most)),
            pltpu.SemaphoreType.DMA((3, most)),
        ],
        compiler_params=pltpu.CompilerParams(collective_id=0, has_side_effects=True),
    )(partial)


def orthonormalize(rows, count):
    partial = jnp.dot(rows, rows.T, precision=lax.Precision.HIGHEST)
    factor, inverse = factor_and_inverse(partial, count)
    return (jnp.dot(inverse.T, rows, precision=lax.Precision.HIGHEST), factor)


def body(rhs, coef_x, coef_y, coef_z, diag_term):
    up_z, lo_z = face_coefs(coef_z, "gz", 0)
    up_x, lo_x = face_coefs(coef_x, "gx", 1)
    up_y, lo_y = face_coefs(coef_y, "gy", 2)
    blocks = [rhs]
    field = rhs
    for section in range(STEPS):
        bz, az = neighbours(field, "gz", 1)
        bx, ax = neighbours(field, "gx", 2)
        by, ay = neighbours(field, "gy", 3)
        mz, pz = shifted(field, 1, bz, az)
        mx, px = shifted(field, 2, bx, ax)
        my, py = shifted(field, 3, by, ay)
        center = field
        image = diag_term * center
        image = image + (up_z * (center - pz) + lo_z * (center - mz))
        image = image + (up_x * (center - px) + lo_x * (center - mx))
        image = image + (up_y * (center - py) + lo_y * (center - my))
        field = (image - NEWTON_SHIFTS[section] * field) * BASIS_SCALE
        blocks.append(field)
    basis = jnp.concatenate(blocks, 0)
    rows = basis.reshape(basis.shape[0], -1)
    count = float(rows.shape[1] * lax.axis_size("gx") * lax.axis_size("gy") * lax.axis_size("gz"))
    first, factor_one = orthonormalize(rows, count)
    second, factor_two = orthonormalize(first, count)
    return (
        second.reshape(basis.shape),
        jnp.dot(factor_two, factor_one, precision=lax.Precision.HIGHEST),
    )


def solution(mesh):
    return jax.shard_map(
        body,
        mesh=mesh,
        in_specs=(
            P(None, "gz", "gx", "gy"),
            P("gz", "gx", "gy"),
            P("gz", "gx", "gy"),
            P("gz", "gx", "gy"),
            P("gz", "gx", "gy"),
        ),
        out_specs=(P(None, "gz", "gx", "gy"), P()),
        check_vma=False,
    )
```

```python
import jax
import jax.numpy as jnp
from jax import lax
import functools
from jax.experimental import pallas as pl
from jax.experimental.pallas import tpu as pltpu
from jax.sharding import PartitionSpec as P

STEPS = 4


NEWTON_SHIFTS = (3.0, 11.0, 7.0, 1.5)
BASIS_SCALE = 1.0 / 6.0
AXES = ("gx", "gy", "gz")


def neighbours(value, axis_name, dim):
    count = lax.axis_size(axis_name)
    length = value.shape[dim]
    up = [(i, i + 1) for i in range(count - 1)]
    down = [(i + 1, i) for i in range(count - 1)]
    last = lax.slice_in_dim(value, length - 1, length, axis=dim)
    first = lax.slice_in_dim(value, 0, 1, axis=dim)
    below = lax.ppermute(last, axis_name, up)
    above = lax.ppermute(first, axis_name, down)
    return below, above


def shifted(value, dim, below, above):
    length = value.shape[dim]
    minus = jnp.concatenate([below, lax.slice_in_dim(value, 0, length - 1, axis=dim)], axis=dim)
    plus = jnp.concatenate([lax.slice_in_dim(value, 1, length, axis=dim), above], axis=dim)
    return minus, plus


def face_coefs(coef, dim, below, above):
    minus, plus = shifted(coef, dim, below, above)
    return 0.5 * (coef + plus), 0.5 * (coef + minus)


def neighbours_with_coef(field, coef, axis_name, dim):
    lead = field.shape[0]
    count = lax.axis_size(axis_name)
    length = field.shape[dim]
    up = [(i, i + 1) for i in range(count - 1)]
    down = [(i + 1, i) for i in range(count - 1)]
    last = jnp.concatenate([
        lax.slice_in_dim(field, length - 1, length, axis=dim),
        lax.slice_in_dim(coef, length - 1, length, axis=dim - 1)[None],
    ], 0)
    first = jnp.concatenate([
        lax.slice_in_dim(field, 0, 1, axis=dim),
        lax.slice_in_dim(coef, 0, 1, axis=dim - 1)[None],
    ], 0)
    below = lax.ppermute(last, axis_name, up)
    above = lax.ppermute(first, axis_name, down)
    field_faces = (below[:lead], above[:lead])
    coef_faces = face_coefs(coef, dim - 1, below[lead], above[lead])
    return field_faces, coef_faces


def cholesky_and_inverse(a, r_ref, x_ref):
    n = a.shape[0]
    rows = lax.broadcasted_iota(jnp.int32, (n, n), 0)
    cols = lax.broadcasted_iota(jnp.int32, (n, n), 1)
    lane = cols[0:1, :]
    sub = rows[:, 0:1]
    r = jnp.zeros((n, n), jnp.float32)
    rt = jnp.zeros((n, n), jnp.float32)
    pivots = []
    for k in range(n):
        rowk = jnp.sum(jnp.where(rows == k, a, 0.0), axis=0, keepdims=True)
        colk = jnp.sum(jnp.where(cols == k, a, 0.0), axis=1, keepdims=True)
        piv = jnp.sqrt(jnp.sum(jnp.where(lane == k, rowk, 0.0), axis=1, keepdims=True))
        rrow = jnp.where(lane >= k, rowk / piv, 0.0)
        rcol = jnp.where(sub >= k, colk / piv, 0.0)
        r = jnp.where(rows == k, rrow, r)
        rt = jnp.where(cols == k, rcol, rt)
        a = a - rcol * rrow
        pivots.append(piv)
    x = jnp.zeros((n, n), jnp.float32)
    for i in range(n - 1, -1, -1):
        ident = jnp.where(lane == i, 1.0, 0.0)
        if i < n - 1:
            c = jnp.sum(jnp.where(cols == i, rt, 0.0), axis=1, keepdims=True)
            s = jnp.sum(jnp.where(sub > i, c * x, 0.0), axis=0, keepdims=True)
            ident = ident - s
        x = jnp.where(rows == i, ident / pivots[i], x)
    r_ref[...] = r
    x_ref[...] = x


def gram_kernel(sizes, count, g_ref, r_ref, x_ref, bx, by, bz, s1, s2, send_sem, recv_sem):
    bufs = (bx, by, bz)
    me = tuple(lax.axis_index(a) for a in AXES)

    def device(axis, index):
        return tuple(index if j == axis else me[j] for j in range(3))

    for buf in bufs:
        buf[...] = jnp.zeros_like(buf)
    barrier = pltpu.get_barrier_semaphore()
    peers = 0
    for axis in range(3):
        n = sizes[axis]
        for d in range(1, n):
            pl.semaphore_signal(barrier, inc=1, device_id=device(axis, (me[axis] + d) % n), device_id_type=pl.DeviceIdType.MESH)
            peers += 1
    pl.semaphore_wait(barrier, peers)

    src = g_ref
    total = None
    for axis, dst in zip(range(3), (s1, s2, None)):
        n = sizes[axis]
        m = me[axis]
        buf = bufs[axis]
        sends = []
        for d in range(1, n):
            copy = pltpu.make_async_remote_copy(
                src_ref=src,
                dst_ref=buf.at[m],
                send_sem=send_sem.at[axis, d],
                recv_sem=recv_sem.at[axis, m],
                device_id=device(axis, (m + d) % n),
                device_id_type=pl.DeviceIdType.MESH,
            )
            copy.start()
            sends.append(copy)
        for d in range(1, n):
            q = (m + n - d) % n
            pltpu.make_async_remote_copy(
                src_ref=src,
                dst_ref=buf.at[q],
                send_sem=send_sem.at[axis, d],
                recv_sem=recv_sem.at[axis, q],
                device_id=device(axis, q),
                device_id_type=pl.DeviceIdType.MESH,
            ).wait_recv()
        own = src[...]
        total = None
        for slot in range(n):
            value = jnp.where(m == slot, own, buf[slot])
            total = value if total is None else total + value
        for copy in sends:
            copy.wait_send()
        if dst is not None:
            dst[...] = total
            src = dst
    cholesky_and_inverse(total / count, r_ref, x_ref)


def factor_and_inverse(partial, count):
    n = partial.shape[0]
    sizes = tuple(lax.axis_size(a) for a in AXES)
    most = max(sizes)
    return pl.pallas_call(
        functools.partial(gram_kernel, sizes, count),
        out_shape=(
            jax.ShapeDtypeStruct((n, n), jnp.float32),
            jax.ShapeDtypeStruct((n, n), jnp.float32),
        ),
        scratch_shapes=[
            pltpu.VMEM((sizes[0], n, n), jnp.float32),
            pltpu.VMEM((sizes[1], n, n), jnp.float32),
            pltpu.VMEM((sizes[2], n, n), jnp.float32),
            pltpu.VMEM((n, n), jnp.float32),
            pltpu.VMEM((n, n), jnp.float32),
            pltpu.SemaphoreType.DMA((3, most)),
            pltpu.SemaphoreType.DMA((3, most)),
        ],
        compiler_params=pltpu.CompilerParams(collective_id=0, has_side_effects=True),
    )(partial)


def orthonormalize(rows, count):
    partial = jnp.dot(rows, rows.T, precision=lax.Precision.HIGHEST)
    factor, inverse = factor_and_inverse(partial, count)
    return (jnp.dot(inverse.T, rows, precision=lax.Precision.HIGHEST), factor)


def body(rhs, coef_x, coef_y, coef_z, diag_term):
    (bz, az), (up_z, lo_z) = neighbours_with_coef(rhs, coef_z, "gz", 1)
    (bx, ax), (up_x, lo_x) = neighbours_with_coef(rhs, coef_x, "gx", 2)
    (by, ay), (up_y, lo_y) = neighbours_with_coef(rhs, coef_y, "gy", 3)
    blocks = [rhs]
    field = rhs
    for section in range(STEPS):
        if section > 0:
            bz, az = neighbours(field, "gz", 1)
            bx, ax = neighbours(field, "gx", 2)
            by, ay = neighbours(field, "gy", 3)
        mz, pz = shifted(field, 1, bz, az)
        mx, px = shifted(field, 2, bx, ax)
        my, py = shifted(field, 3, by, ay)
        center = field
        image = diag_term * center
        image = image + (up_z * (center - pz) + lo_z * (center - mz))
        image = image + (up_x * (center - px) + lo_x * (center - mx))
        image = image + (up_y * (center - py) + lo_y * (center - my))
        field = (image - NEWTON_SHIFTS[section] * field) * BASIS_SCALE
        blocks.append(field)
    basis = jnp.concatenate(blocks, 0)
    rows = basis.reshape(basis.shape[0], -1)
    count = float(rows.shape[1] * lax.axis_size("gx") * lax.axis_size("gy") * lax.axis_size("gz"))
    first, factor_one = orthonormalize(rows, count)
    second, factor_two = orthonormalize(first, count)
    return (
        second.reshape(basis.shape),
        jnp.dot(factor_two, factor_one, precision=lax.Precision.HIGHEST),
    )


def solution(mesh):
    return jax.shard_map(
        body,
        mesh=mesh,
        in_specs=(
            P(None, "gz", "gx", "gy"),
            P("gz", "gx", "gy"),
            P("gz", "gx", "gy"),
            P("gz", "gx", "gy"),
            P("gz", "gx", "gy"),
        ),
        out_specs=(P(None, "gz", "gx", "gy"), P()),
        check_vma=False,
    )
```

```python
import jax
import jax.numpy as jnp
from jax import lax
import functools
from jax.experimental import pallas as pl
from jax.experimental.pallas import tpu as pltpu
from jax.sharding import PartitionSpec as P

STEPS = 4


NEWTON_SHIFTS = (3.0, 11.0, 7.0, 1.5)
BASIS_SCALE = 1.0 / 6.0
AXES = ("gx", "gy", "gz")


def halo_kernel(sizes, *refs):
    faces = refs[0:6]
    outs = refs[6:12]
    send_sem, recv_sem = refs[12], refs[13]
    me = tuple(lax.axis_index(a) for a in AXES)

    def device(axis, index):
        return tuple(index if j == axis else me[j] for j in range(3))

    barrier = pltpu.get_barrier_semaphore()
    for axis in range(3):
        n = sizes[axis]
        for step in (1, n - 1):
            pl.semaphore_signal(barrier, inc=1, device_id=device(axis, (me[axis] + step) % n), device_id_type=pl.DeviceIdType.MESH)
    pl.semaphore_wait(barrier, 6)
    copies = []
    for axis in range(3):
        n = sizes[axis]
        last, first = faces[2 * axis], faces[2 * axis + 1]
        below, above = outs[2 * axis], outs[2 * axis + 1]
        for k, (src, dst, step) in enumerate(((last, below, 1), (first, above, n - 1))):
            copy = pltpu.make_async_remote_copy(
                src_ref=src,
                dst_ref=dst,
                send_sem=send_sem.at[axis, k],
                recv_sem=recv_sem.at[axis, k],
                device_id=device(axis, (me[axis] + step) % n),
                device_id_type=pl.DeviceIdType.MESH,
            )
            copy.start()
            copies.append(copy)
    for copy in copies:
        copy.wait()


def exchange(faces, collective_id):
    sizes = tuple(lax.axis_size(a) for a in AXES)
    flat = [f for pair in faces for f in pair]
    outs = pl.pallas_call(
        functools.partial(halo_kernel, sizes),
        out_shape=tuple(jax.ShapeDtypeStruct(f.shape, f.dtype) for f in flat),
        scratch_shapes=[pltpu.SemaphoreType.DMA((3, 2)), pltpu.SemaphoreType.DMA((3, 2))],
        compiler_params=pltpu.CompilerParams(collective_id=collective_id, has_side_effects=True),
    )(*flat)
    result = []
    for axis, name in enumerate(AXES):
        m = lax.axis_index(name)
        n = sizes[axis]
        below = jnp.where(m == 0, 0.0, outs[2 * axis])
        above = jnp.where(m == n - 1, 0.0, outs[2 * axis + 1])
        result.append((below, above))
    return result


def end_faces(value, dim):
    length = value.shape[dim]
    return (lax.slice_in_dim(value, length - 1, length, axis=dim), lax.slice_in_dim(value, 0, 1, axis=dim))


def shifted(value, dim, below, above):
    length = value.shape[dim]
    minus = jnp.concatenate([below, lax.slice_in_dim(value, 0, length - 1, axis=dim)], axis=dim)
    plus = jnp.concatenate([lax.slice_in_dim(value, 1, length, axis=dim), above], axis=dim)
    return minus, plus


def face_coefs(coef, dim, below, above):
    minus, plus = shifted(coef, dim, below, above)
    return 0.5 * (coef + plus), 0.5 * (coef + minus)


def cholesky_and_inverse(a, r_ref, x_ref):
    n = a.shape[0]
    rows = lax.broadcasted_iota(jnp.int32, (n, n), 0)
    cols = lax.broadcasted_iota(jnp.int32, (n, n), 1)
    lane = cols[0:1, :]
    sub = rows[:, 0:1]
    r = jnp.zeros((n, n), jnp.float32)
    rt = jnp.zeros((n, n), jnp.float32)
    pivots = []
    for k in range(n):
        rowk = jnp.sum(jnp.where(rows == k, a, 0.0), axis=0, keepdims=True)
        colk = jnp.sum(jnp.where(cols == k, a, 0.0), axis=1, keepdims=True)
        piv = jnp.sqrt(jnp.sum(jnp.where(lane == k, rowk, 0.0), axis=1, keepdims=True))
        rrow = jnp.where(lane >= k, rowk / piv, 0.0)
        rcol = jnp.where(sub >= k, colk / piv, 0.0)
        r = jnp.where(rows == k, rrow, r)
        rt = jnp.where(cols == k, rcol, rt)
        a = a - rcol * rrow
        pivots.append(piv)
    x = jnp.zeros((n, n), jnp.float32)
    for i in range(n - 1, -1, -1):
        ident = jnp.where(lane == i, 1.0, 0.0)
        if i < n - 1:
            c = jnp.sum(jnp.where(cols == i, rt, 0.0), axis=1, keepdims=True)
            s = jnp.sum(jnp.where(sub > i, c * x, 0.0), axis=0, keepdims=True)
            ident = ident - s
        x = jnp.where(rows == i, ident / pivots[i], x)
    r_ref[...] = r
    x_ref[...] = x


def gram_kernel(sizes, count, g_ref, r_ref, x_ref, bx, by, bz, s1, s2, send_sem, recv_sem):
    bufs = (bx, by, bz)
    me = tuple(lax.axis_index(a) for a in AXES)

    def device(axis, index):
        return tuple(index if j == axis else me[j] for j in range(3))

    for buf in bufs:
        buf[...] = jnp.zeros_like(buf)
    barrier = pltpu.get_barrier_semaphore()
    peers = 0
    for axis in range(3):
        n = sizes[axis]
        for d in range(1, n):
            pl.semaphore_signal(barrier, inc=1, device_id=device(axis, (me[axis] + d) % n), device_id_type=pl.DeviceIdType.MESH)
            peers += 1
    pl.semaphore_wait(barrier, peers)

    src = g_ref
    total = None
    for axis, dst in zip(range(3), (s1, s2, None)):
        n = sizes[axis]
        m = me[axis]
        buf = bufs[axis]
        sends = []
        for d in range(1, n):
            copy = pltpu.make_async_remote_copy(
                src_ref=src,
                dst_ref=buf.at[m],
                send_sem=send_sem.at[axis, d],
                recv_sem=recv_sem.at[axis, m],
                device_id=device(axis, (m + d) % n),
                device_id_type=pl.DeviceIdType.MESH,
            )
            copy.start()
            sends.append(copy)
        for d in range(1, n):
            q = (m + n - d) % n
            pltpu.make_async_remote_copy(
                src_ref=src,
                dst_ref=buf.at[q],
                send_sem=send_sem.at[axis, d],
                recv_sem=recv_sem.at[axis, q],
                device_id=device(axis, q),
                device_id_type=pl.DeviceIdType.MESH,
            ).wait_recv()
        own = src[...]
        total = None
        for slot in range(n):
            value = jnp.where(m == slot, own, buf[slot])
            total = value if total is None else total + value
        for copy in sends:
            copy.wait_send()
        if dst is not None:
            dst[...] = total
            src = dst
    cholesky_and_inverse(total / count, r_ref, x_ref)


def factor_and_inverse(partial, count):
    n = partial.shape[0]
    sizes = tuple(lax.axis_size(a) for a in AXES)
    most = max(sizes)
    return pl.pallas_call(
        functools.partial(gram_kernel, sizes, count),
        out_shape=(
            jax.ShapeDtypeStruct((n, n), jnp.float32),
            jax.ShapeDtypeStruct((n, n), jnp.float32),
        ),
        scratch_shapes=[
            pltpu.VMEM((sizes[0], n, n), jnp.float32),
            pltpu.VMEM((sizes[1], n, n), jnp.float32),
            pltpu.VMEM((sizes[2], n, n), jnp.float32),
            pltpu.VMEM((n, n), jnp.float32),
            pltpu.VMEM((n, n), jnp.float32),
            pltpu.SemaphoreType.DMA((3, most)),
            pltpu.SemaphoreType.DMA((3, most)),
        ],
        compiler_params=pltpu.CompilerParams(collective_id=0, has_side_effects=True),
    )(partial)


def orthonormalize(rows, count):
    partial = jnp.dot(rows, rows.T, precision=lax.Precision.HIGHEST)
    factor, inverse = factor_and_inverse(partial, count)
    return (jnp.dot(inverse.T, rows, precision=lax.Precision.HIGHEST), factor)


def body(rhs, coef_x, coef_y, coef_z, diag_term):
    coefs = (coef_x, coef_y, coef_z)
    faces = []
    for axis, dim in enumerate((2, 3, 1)):
        last_f, first_f = end_faces(rhs, dim)
        last_c, first_c = end_faces(coefs[axis], dim - 1)
        faces.append((jnp.concatenate([last_f, last_c[None]], 0), jnp.concatenate([first_f, first_c[None]], 0)))
    got = exchange(faces, 1)
    lead = rhs.shape[0]
    (bx, ax), (by, ay), (bz, az) = [(b[:lead], a[:lead]) for b, a in got]
    up_x, lo_x = face_coefs(coef_x, 1, got[0][0][lead], got[0][1][lead])
    up_y, lo_y = face_coefs(coef_y, 2, got[1][0][lead], got[1][1][lead])
    up_z, lo_z = face_coefs(coef_z, 0, got[2][0][lead], got[2][1][lead])
    blocks = [rhs]
    field = rhs
    for section in range(STEPS):
        if section > 0:
            (bx, ax), (by, ay), (bz, az) = exchange([end_faces(field, d) for d in (2, 3, 1)], 2)
        mz, pz = shifted(field, 1, bz, az)
        mx, px = shifted(field, 2, bx, ax)
        my, py = shifted(field, 3, by, ay)
        center = field
        image = diag_term * center
        image = image + (up_z * (center - pz) + lo_z * (center - mz))
        image = image + (up_x * (center - px) + lo_x * (center - mx))
        image = image + (up_y * (center - py) + lo_y * (center - my))
        field = (image - NEWTON_SHIFTS[section] * field) * BASIS_SCALE
        blocks.append(field)
    basis = jnp.concatenate(blocks, 0)
    rows = basis.reshape(basis.shape[0], -1)
    count = float(rows.shape[1] * lax.axis_size("gx") * lax.axis_size("gy") * lax.axis_size("gz"))
    first, factor_one = orthonormalize(rows, count)
    second, factor_two = orthonormalize(first, count)
    return (
        second.reshape(basis.shape),
        jnp.dot(factor_two, factor_one, precision=lax.Precision.HIGHEST),
    )


def solution(mesh):
    return jax.shard_map(
        body,
        mesh=mesh,
        in_specs=(
            P(None, "gz", "gx", "gy"),
            P("gz", "gx", "gy"),
            P("gz", "gx", "gy"),
            P("gz", "gx", "gy"),
            P("gz", "gx", "gy"),
        ),
        out_specs=(P(None, "gz", "gx", "gy"), P()),
        check_vma=False,
    )
```

```python
import jax
import jax.numpy as jnp
from jax import lax
import functools
from jax.experimental import pallas as pl
from jax.experimental.pallas import tpu as pltpu
from jax.sharding import PartitionSpec as P

STEPS = 4


NEWTON_SHIFTS = (3.0, 11.0, 7.0, 1.5)
BASIS_SCALE = 1.0 / 6.0
AXES = ("gx", "gy", "gz")


def halo_kernel(sizes, *refs):
    faces = refs[0:6]
    outs = refs[6:12]
    send_sem, recv_sem = refs[12], refs[13]
    me = tuple(lax.axis_index(a) for a in AXES)

    def device(axis, index):
        return tuple(index if j == axis else me[j] for j in range(3))

    barrier = pltpu.get_barrier_semaphore()
    for axis in range(3):
        n = sizes[axis]
        for step in (1, n - 1):
            pl.semaphore_signal(barrier, inc=1, device_id=device(axis, (me[axis] + step) % n), device_id_type=pl.DeviceIdType.MESH)
    pl.semaphore_wait(barrier, 6)
    copies = []
    for axis in range(3):
        n = sizes[axis]
        last, first = faces[2 * axis], faces[2 * axis + 1]
        below, above = outs[2 * axis], outs[2 * axis + 1]
        for k, (src, dst, step) in enumerate(((last, below, 1), (first, above, n - 1))):
            copy = pltpu.make_async_remote_copy(
                src_ref=src,
                dst_ref=dst,
                send_sem=send_sem.at[axis, k],
                recv_sem=recv_sem.at[axis, k],
                device_id=device(axis, (me[axis] + step) % n),
                device_id_type=pl.DeviceIdType.MESH,
            )
            copy.start()
            copies.append(copy)
    for copy in copies:
        copy.wait()


def exchange(faces, collective_id):
    sizes = tuple(lax.axis_size(a) for a in AXES)
    flat = [f for pair in faces for f in pair]
    outs = pl.pallas_call(
        functools.partial(halo_kernel, sizes),
        out_shape=tuple(jax.ShapeDtypeStruct(f.shape, f.dtype) for f in flat),
        scratch_shapes=[pltpu.SemaphoreType.DMA((3, 2)), pltpu.SemaphoreType.DMA((3, 2))],
        compiler_params=pltpu.CompilerParams(collective_id=collective_id, has_side_effects=True),
    )(*flat)
    result = []
    for axis, name in enumerate(AXES):
        m = lax.axis_index(name)
        n = sizes[axis]
        below = jnp.where(m == 0, 0.0, outs[2 * axis])
        above = jnp.where(m == n - 1, 0.0, outs[2 * axis + 1])
        result.append((below, above))
    return result


def end_faces(value, dim):
    length = value.shape[dim]
    return (lax.slice_in_dim(value, length - 1, length, axis=dim), lax.slice_in_dim(value, 0, 1, axis=dim))


def shifted(value, dim, below, above):
    length = value.shape[dim]
    minus = jnp.concatenate([below, lax.slice_in_dim(value, 0, length - 1, axis=dim)], axis=dim)
    plus = jnp.concatenate([lax.slice_in_dim(value, 1, length, axis=dim), above], axis=dim)
    return minus, plus


def face_coefs(coef, dim, below, above):
    minus, plus = shifted(coef, dim, below, above)
    return 0.5 * (coef + plus), 0.5 * (coef + minus)


def cholesky_and_inverse(a, r_ref, x_ref):
    n = a.shape[0]
    rows = lax.broadcasted_iota(jnp.int32, (n, n), 0)
    cols = lax.broadcasted_iota(jnp.int32, (n, n), 1)
    lane = cols[0:1, :]
    sub = rows[:, 0:1]
    r = jnp.zeros((n, n), jnp.float32)
    rt = jnp.zeros((n, n), jnp.float32)
    pivots = []
    for k in range(n):
        rowk = jnp.sum(jnp.where(rows == k, a, 0.0), axis=0, keepdims=True)
        colk = jnp.sum(jnp.where(cols == k, a, 0.0), axis=1, keepdims=True)
        piv = jnp.sqrt(jnp.sum(jnp.where(lane == k, rowk, 0.0), axis=1, keepdims=True))
        rrow = jnp.where(lane >= k, rowk / piv, 0.0)
        rcol = jnp.where(sub >= k, colk / piv, 0.0)
        r = jnp.where(rows == k, rrow, r)
        rt = jnp.where(cols == k, rcol, rt)
        a = a - rcol * rrow
        pivots.append(piv)
    x = jnp.zeros((n, n), jnp.float32)
    for i in range(n - 1, -1, -1):
        ident = jnp.where(lane == i, 1.0, 0.0)
        if i < n - 1:
            c = jnp.sum(jnp.where(cols == i, rt, 0.0), axis=1, keepdims=True)
            s = jnp.sum(jnp.where(sub > i, c * x, 0.0), axis=0, keepdims=True)
            ident = ident - s
        x = jnp.where(rows == i, ident / pivots[i], x)
    r_ref[...] = r
    x_ref[...] = x


def gram_kernel(sizes, count, g_ref, r_ref, x_ref, bxy, bz, s1, send_sem, recv_sem):
    me = tuple(lax.axis_index(a) for a in AXES)
    span = sizes[1]
    groups = (
        (sizes[0] * sizes[1], me[0] * span + me[1], lambda p: (p // span, p % span, me[2]), bxy),
        (sizes[2], me[2], lambda p: (me[0], me[1], p), bz),
    )
    for group in groups:
        group[3][...] = jnp.zeros_like(group[3])
    barrier = pltpu.get_barrier_semaphore()
    peers = 0
    for n, m, device, _ in groups:
        for d in range(1, n):
            pl.semaphore_signal(barrier, inc=1, device_id=device((m + d) % n), device_id_type=pl.DeviceIdType.MESH)
            peers += 1
    pl.semaphore_wait(barrier, peers)

    src = g_ref
    total = None
    for g, ((n, m, device, buf), dst) in enumerate(zip(groups, (s1, None))):
        sends = []
        for d in range(1, n):
            copy = pltpu.make_async_remote_copy(
                src_ref=src,
                dst_ref=buf.at[m],
                send_sem=send_sem.at[g, d],
                recv_sem=recv_sem.at[g, m],
                device_id=device((m + d) % n),
                device_id_type=pl.DeviceIdType.MESH,
            )
            copy.start()
            sends.append(copy)
        for d in range(1, n):
            q = (m + n - d) % n
            pltpu.make_async_remote_copy(
                src_ref=src,
                dst_ref=buf.at[q],
                send_sem=send_sem.at[g, d],
                recv_sem=recv_sem.at[g, q],
                device_id=device(q),
                device_id_type=pl.DeviceIdType.MESH,
            ).wait_recv()
        own = src[...]
        total = None
        for slot in range(n):
            value = jnp.where(m == slot, own, buf[slot])
            total = value if total is None else total + value
        for copy in sends:
            copy.wait_send()
        if dst is not None:
            dst[...] = total
            src = dst
    cholesky_and_inverse(total / count, r_ref, x_ref)


def factor_and_inverse(partial, count):
    n = partial.shape[0]
    sizes = tuple(lax.axis_size(a) for a in AXES)
    most = max(sizes[0] * sizes[1], sizes[2])
    return pl.pallas_call(
        functools.partial(gram_kernel, sizes, count),
        out_shape=(
            jax.ShapeDtypeStruct((n, n), jnp.float32),
            jax.ShapeDtypeStruct((n, n), jnp.float32),
        ),
        scratch_shapes=[
            pltpu.VMEM((sizes[0] * sizes[1], n, n), jnp.float32),
            pltpu.VMEM((sizes[2], n, n), jnp.float32),
            pltpu.VMEM((n, n), jnp.float32),
            pltpu.SemaphoreType.DMA((2, most)),
            pltpu.SemaphoreType.DMA((2, most)),
        ],
        compiler_params=pltpu.CompilerParams(collective_id=0, has_side_effects=True),
    )(partial)


def orthonormalize(rows, count):
    partial = jnp.dot(rows, rows.T, precision=lax.Precision.HIGHEST)
    factor, inverse = factor_and_inverse(partial, count)
    return (jnp.dot(inverse.T, rows, precision=lax.Precision.HIGHEST), factor)


def body(rhs, coef_x, coef_y, coef_z, diag_term):
    coefs = (coef_x, coef_y, coef_z)
    faces = []
    for axis, dim in enumerate((2, 3, 1)):
        last_f, first_f = end_faces(rhs, dim)
        last_c, first_c = end_faces(coefs[axis], dim - 1)
        faces.append((jnp.concatenate([last_f, last_c[None]], 0), jnp.concatenate([first_f, first_c[None]], 0)))
    got = exchange(faces, 1)
    lead = rhs.shape[0]
    (bx, ax), (by, ay), (bz, az) = [(b[:lead], a[:lead]) for b, a in got]
    up_x, lo_x = face_coefs(coef_x, 1, got[0][0][lead], got[0][1][lead])
    up_y, lo_y = face_coefs(coef_y, 2, got[1][0][lead], got[1][1][lead])
    up_z, lo_z = face_coefs(coef_z, 0, got[2][0][lead], got[2][1][lead])
    blocks = [rhs]
    field = rhs
    for section in range(STEPS):
        if section > 0:
            (bx, ax), (by, ay), (bz, az) = exchange([end_faces(field, d) for d in (2, 3, 1)], 2)
        mz, pz = shifted(field, 1, bz, az)
        mx, px = shifted(field, 2, bx, ax)
        my, py = shifted(field, 3, by, ay)
        center = field
        image = diag_term * center
        image = image + (up_z * (center - pz) + lo_z * (center - mz))
        image = image + (up_x * (center - px) + lo_x * (center - mx))
        image = image + (up_y * (center - py) + lo_y * (center - my))
        field = (image - NEWTON_SHIFTS[section] * field) * BASIS_SCALE
        blocks.append(field)
    basis = jnp.concatenate(blocks, 0)
    rows = basis.reshape(basis.shape[0], -1)
    count = float(rows.shape[1] * lax.axis_size("gx") * lax.axis_size("gy") * lax.axis_size("gz"))
    first, factor_one = orthonormalize(rows, count)
    second, factor_two = orthonormalize(first, count)
    return (
        second.reshape(basis.shape),
        jnp.dot(factor_two, factor_one, precision=lax.Precision.HIGHEST),
    )


def solution(mesh):
    return jax.shard_map(
        body,
        mesh=mesh,
        in_specs=(
            P(None, "gz", "gx", "gy"),
            P("gz", "gx", "gy"),
            P("gz", "gx", "gy"),
            P("gz", "gx", "gy"),
            P("gz", "gx", "gy"),
        ),
        out_specs=(P(None, "gz", "gx", "gy"), P()),
        check_vma=False,
    )
```

```python
import jax
import jax.numpy as jnp
from jax import lax
import functools
from jax.experimental import pallas as pl
from jax.experimental.pallas import tpu as pltpu
from jax.sharding import PartitionSpec as P

STEPS = 4


NEWTON_SHIFTS = (3.0, 11.0, 7.0, 1.5)
BASIS_SCALE = 1.0 / 6.0
AXES = ("gx", "gy", "gz")


def halo_kernel(sizes, *refs):
    faces = refs[0:6]
    outs = refs[6:12]
    send_sem, recv_sem = refs[12], refs[13]
    me = tuple(lax.axis_index(a) for a in AXES)

    def device(axis, index):
        return tuple(index if j == axis else me[j] for j in range(3))

    barrier = pltpu.get_barrier_semaphore()
    for axis in range(3):
        n = sizes[axis]
        for step in (1, n - 1):
            pl.semaphore_signal(barrier, inc=1, device_id=device(axis, (me[axis] + step) % n), device_id_type=pl.DeviceIdType.MESH)
    pl.semaphore_wait(barrier, 6)
    copies = []
    for axis in range(3):
        n = sizes[axis]
        last, first = faces[2 * axis], faces[2 * axis + 1]
        below, above = outs[2 * axis], outs[2 * axis + 1]
        for k, (src, dst, step) in enumerate(((last, below, 1), (first, above, n - 1))):
            copy = pltpu.make_async_remote_copy(
                src_ref=src,
                dst_ref=dst,
                send_sem=send_sem.at[axis, k],
                recv_sem=recv_sem.at[axis, k],
                device_id=device(axis, (me[axis] + step) % n),
                device_id_type=pl.DeviceIdType.MESH,
            )
            copy.start()
            copies.append(copy)
    for copy in copies:
        copy.wait()


def exchange(faces, collective_id):
    sizes = tuple(lax.axis_size(a) for a in AXES)
    flat = [f for pair in faces for f in pair]
    outs = pl.pallas_call(
        functools.partial(halo_kernel, sizes),
        out_shape=tuple(jax.ShapeDtypeStruct(f.shape, f.dtype) for f in flat),
        scratch_shapes=[pltpu.SemaphoreType.DMA((3, 2)), pltpu.SemaphoreType.DMA((3, 2))],
        compiler_params=pltpu.CompilerParams(collective_id=collective_id, has_side_effects=True),
    )(*flat)
    result = []
    for axis, name in enumerate(AXES):
        m = lax.axis_index(name)
        n = sizes[axis]
        below = jnp.where(m == 0, 0.0, outs[2 * axis])
        above = jnp.where(m == n - 1, 0.0, outs[2 * axis + 1])
        result.append((below, above))
    return result


def end_faces(value, dim):
    length = value.shape[dim]
    return (lax.slice_in_dim(value, length - 1, length, axis=dim), lax.slice_in_dim(value, 0, 1, axis=dim))


def shifted(value, dim, below, above):
    length = value.shape[dim]
    minus = jnp.concatenate([below, lax.slice_in_dim(value, 0, length - 1, axis=dim)], axis=dim)
    plus = jnp.concatenate([lax.slice_in_dim(value, 1, length, axis=dim), above], axis=dim)
    return minus, plus


def face_coefs(coef, dim, below, above):
    minus, plus = shifted(coef, dim, below, above)
    return 0.5 * (coef + plus), 0.5 * (coef + minus)


def cholesky_and_inverse(a, r_ref, x_ref):
    n = a.shape[0]
    rows = lax.broadcasted_iota(jnp.int32, (n, n), 0)
    cols = lax.broadcasted_iota(jnp.int32, (n, n), 1)
    lane = cols[0:1, :]
    sub = rows[:, 0:1]

    def factor_step(k, carry):
        a, r, rt, diag = carry
        rowk = jnp.sum(jnp.where(rows == k, a, 0.0), axis=0, keepdims=True)
        colk = jnp.sum(jnp.where(cols == k, a, 0.0), axis=1, keepdims=True)
        piv = jnp.sqrt(jnp.sum(jnp.where(lane == k, rowk, 0.0), axis=1, keepdims=True))
        rrow = jnp.where(lane >= k, rowk / piv, 0.0)
        rcol = jnp.where(sub >= k, colk / piv, 0.0)
        r = jnp.where(rows == k, rrow, r)
        rt = jnp.where(cols == k, rcol, rt)
        diag = jnp.where(lane == k, piv, diag)
        return a - rcol * rrow, r, rt, diag

    zeros = jnp.zeros((n, n), jnp.float32)
    _, r, rt, diag = lax.fori_loop(0, n, factor_step, (a, zeros, zeros, jnp.zeros((1, n), jnp.float32)))

    def solve_step(j, x):
        i = n - 1 - j
        ident = jnp.where(lane == i, 1.0, 0.0)
        c = jnp.sum(jnp.where(cols == i, rt, 0.0), axis=1, keepdims=True)
        s = jnp.sum(jnp.where(sub > i, c * x, 0.0), axis=0, keepdims=True)
        piv = jnp.sum(jnp.where(lane == i, diag, 0.0), axis=1, keepdims=True)
        return jnp.where(rows == i, (ident - s) / piv, x)

    x = lax.fori_loop(0, n, solve_step, zeros)
    r_ref[...] = r
    x_ref[...] = x


def gram_kernel(sizes, count, g_ref, r_ref, x_ref, bx, by, bz, s1, s2, send_sem, recv_sem):
    bufs = (bx, by, bz)
    me = tuple(lax.axis_index(a) for a in AXES)

    def device(axis, index):
        return tuple(index if j == axis else me[j] for j in range(3))

    for buf in bufs:
        buf[...] = jnp.zeros_like(buf)
    barrier = pltpu.get_barrier_semaphore()
    peers = 0
    for axis in range(3):
        n = sizes[axis]
        for d in range(1, n):
            pl.semaphore_signal(barrier, inc=1, device_id=device(axis, (me[axis] + d) % n), device_id_type=pl.DeviceIdType.MESH)
            peers += 1
    pl.semaphore_wait(barrier, peers)

    src = g_ref
    total = None
    for axis, dst in zip(range(3), (s1, s2, None)):
        n = sizes[axis]
        m = me[axis]
        buf = bufs[axis]
        sends = []
        for d in range(1, n):
            copy = pltpu.make_async_remote_copy(
                src_ref=src,
                dst_ref=buf.at[m],
                send_sem=send_sem.at[axis, d],
                recv_sem=recv_sem.at[axis, m],
                device_id=device(axis, (m + d) % n),
                device_id_type=pl.DeviceIdType.MESH,
            )
            copy.start()
            sends.append(copy)
        for d in range(1, n):
            q = (m + n - d) % n
            pltpu.make_async_remote_copy(
                src_ref=src,
                dst_ref=buf.at[q],
                send_sem=send_sem.at[axis, d],
                recv_sem=recv_sem.at[axis, q],
                device_id=device(axis, q),
                device_id_type=pl.DeviceIdType.MESH,
            ).wait_recv()
        own = src[...]
        total = None
        for slot in range(n):
            value = jnp.where(m == slot, own, buf[slot])
            total = value if total is None else total + value
        for copy in sends:
            copy.wait_send()
        if dst is not None:
            dst[...] = total
            src = dst
    cholesky_and_inverse(total / count, r_ref, x_ref)


def factor_and_inverse(partial, count):
    n = partial.shape[0]
    sizes = tuple(lax.axis_size(a) for a in AXES)
    most = max(sizes)
    return pl.pallas_call(
        functools.partial(gram_kernel, sizes, count),
        out_shape=(
            jax.ShapeDtypeStruct((n, n), jnp.float32),
            jax.ShapeDtypeStruct((n, n), jnp.float32),
        ),
        scratch_shapes=[
            pltpu.VMEM((sizes[0], n, n), jnp.float32),
            pltpu.VMEM((sizes[1], n, n), jnp.float32),
            pltpu.VMEM((sizes[2], n, n), jnp.float32),
            pltpu.VMEM((n, n), jnp.float32),
            pltpu.VMEM((n, n), jnp.float32),
            pltpu.SemaphoreType.DMA((3, most)),
            pltpu.SemaphoreType.DMA((3, most)),
        ],
        compiler_params=pltpu.CompilerParams(collective_id=0, has_side_effects=True),
    )(partial)


def orthonormalize(rows, count):
    partial = jnp.dot(rows, rows.T, precision=lax.Precision.HIGHEST)
    factor, inverse = factor_and_inverse(partial, count)
    return (jnp.dot(inverse.T, rows, precision=lax.Precision.HIGHEST), factor)


def body(rhs, coef_x, coef_y, coef_z, diag_term):
    coefs = (coef_x, coef_y, coef_z)
    faces = []
    for axis, dim in enumerate((2, 3, 1)):
        last_f, first_f = end_faces(rhs, dim)
        last_c, first_c = end_faces(coefs[axis], dim - 1)
        faces.append((jnp.concatenate([last_f, last_c[None]], 0), jnp.concatenate([first_f, first_c[None]], 0)))
    got = exchange(faces, 1)
    lead = rhs.shape[0]
    (bx, ax), (by, ay), (bz, az) = [(b[:lead], a[:lead]) for b, a in got]
    up_x, lo_x = face_coefs(coef_x, 1, got[0][0][lead], got[0][1][lead])
    up_y, lo_y = face_coefs(coef_y, 2, got[1][0][lead], got[1][1][lead])
    up_z, lo_z = face_coefs(coef_z, 0, got[2][0][lead], got[2][1][lead])
    blocks = [rhs]
    field = rhs
    for section in range(STEPS):
        if section > 0:
            (bx, ax), (by, ay), (bz, az) = exchange([end_faces(field, d) for d in (2, 3, 1)], 2)
        mz, pz = shifted(field, 1, bz, az)
        mx, px = shifted(field, 2, bx, ax)
        my, py = shifted(field, 3, by, ay)
        center = field
        image = diag_term * center
        image = image + (up_z * (center - pz) + lo_z * (center - mz))
        image = image + (up_x * (center - px) + lo_x * (center - mx))
        image = image + (up_y * (center - py) + lo_y * (center - my))
        field = (image - NEWTON_SHIFTS[section] * field) * BASIS_SCALE
        blocks.append(field)
    basis = jnp.concatenate(blocks, 0)
    rows = basis.reshape(basis.shape[0], -1)
    count = float(rows.shape[1] * lax.axis_size("gx") * lax.axis_size("gy") * lax.axis_size("gz"))
    first, factor_one = orthonormalize(rows, count)
    second, factor_two = orthonormalize(first, count)
    return (
        second.reshape(basis.shape),
        jnp.dot(factor_two, factor_one, precision=lax.Precision.HIGHEST),
    )


def solution(mesh):
    return jax.shard_map(
        body,
        mesh=mesh,
        in_specs=(
            P(None, "gz", "gx", "gy"),
            P("gz", "gx", "gy"),
            P("gz", "gx", "gy"),
            P("gz", "gx", "gy"),
            P("gz", "gx", "gy"),
        ),
        out_specs=(P(None, "gz", "gx", "gy"), P()),
        check_vma=False,
    )
```

```python
import jax
import jax.numpy as jnp
from jax import lax
import functools
from jax.experimental import pallas as pl
from jax.experimental.pallas import tpu as pltpu
from jax.sharding import PartitionSpec as P

STEPS = 4


NEWTON_SHIFTS = (3.0, 11.0, 7.0, 1.5)
BASIS_SCALE = 1.0 / 6.0
AXES = ("gx", "gy", "gz")


def halo_kernel(sizes, *refs):
    faces = refs[0:6]
    outs = refs[6:12]
    send_sem, recv_sem = refs[12], refs[13]
    me = tuple(lax.axis_index(a) for a in AXES)

    def device(axis, index):
        return tuple(index if j == axis else me[j] for j in range(3))

    barrier = pltpu.get_barrier_semaphore()
    for axis in range(3):
        n = sizes[axis]
        for step in (1, n - 1):
            pl.semaphore_signal(barrier, inc=1, device_id=device(axis, (me[axis] + step) % n), device_id_type=pl.DeviceIdType.MESH)
    pl.semaphore_wait(barrier, 6)
    copies = []
    for axis in range(3):
        n = sizes[axis]
        last, first = faces[2 * axis], faces[2 * axis + 1]
        below, above = outs[2 * axis], outs[2 * axis + 1]
        for k, (src, dst, step) in enumerate(((last, below, 1), (first, above, n - 1))):
            copy = pltpu.make_async_remote_copy(
                src_ref=src,
                dst_ref=dst,
                send_sem=send_sem.at[axis, k],
                recv_sem=recv_sem.at[axis, k],
                device_id=device(axis, (me[axis] + step) % n),
                device_id_type=pl.DeviceIdType.MESH,
            )
            copy.start()
            copies.append(copy)
    for copy in copies:
        copy.wait()


def exchange(faces, collective_id):
    sizes = tuple(lax.axis_size(a) for a in AXES)
    shapes = [f.shape for pair in faces for f in pair]
    flat = [f.reshape(f.size // 128, 128) for pair in faces for f in pair]
    outs = pl.pallas_call(
        functools.partial(halo_kernel, sizes),
        out_shape=tuple(jax.ShapeDtypeStruct(f.shape, f.dtype) for f in flat),
        scratch_shapes=[pltpu.SemaphoreType.DMA((3, 2)), pltpu.SemaphoreType.DMA((3, 2))],
        compiler_params=pltpu.CompilerParams(collective_id=collective_id, has_side_effects=True),
    )(*flat)
    outs = [o.reshape(shape) for o, shape in zip(outs, shapes)]
    result = []
    for axis, name in enumerate(AXES):
        m = lax.axis_index(name)
        n = sizes[axis]
        below = jnp.where(m == 0, 0.0, outs[2 * axis])
        above = jnp.where(m == n - 1, 0.0, outs[2 * axis + 1])
        result.append((below, above))
    return result


def end_faces(value, dim):
    length = value.shape[dim]
    return (lax.slice_in_dim(value, length - 1, length, axis=dim), lax.slice_in_dim(value, 0, 1, axis=dim))


def shifted(value, dim, below, above):
    length = value.shape[dim]
    minus = jnp.concatenate([below, lax.slice_in_dim(value, 0, length - 1, axis=dim)], axis=dim)
    plus = jnp.concatenate([lax.slice_in_dim(value, 1, length, axis=dim), above], axis=dim)
    return minus, plus


def face_coefs(coef, dim, below, above):
    minus, plus = shifted(coef, dim, below, above)
    return 0.5 * (coef + plus), 0.5 * (coef + minus)


def cholesky_and_inverse(a, r_ref, x_ref):
    n = a.shape[0]
    rows = lax.broadcasted_iota(jnp.int32, (n, n), 0)
    cols = lax.broadcasted_iota(jnp.int32, (n, n), 1)
    lane = cols[0:1, :]
    sub = rows[:, 0:1]
    r = jnp.zeros((n, n), jnp.float32)
    rt = jnp.zeros((n, n), jnp.float32)
    pivots = []
    for k in range(n):
        rowk = jnp.sum(jnp.where(rows == k, a, 0.0), axis=0, keepdims=True)
        colk = jnp.sum(jnp.where(cols == k, a, 0.0), axis=1, keepdims=True)
        piv = jnp.sqrt(jnp.sum(jnp.where(lane == k, rowk, 0.0), axis=1, keepdims=True))
        rrow = jnp.where(lane >= k, rowk / piv, 0.0)
        rcol = jnp.where(sub >= k, colk / piv, 0.0)
        r = jnp.where(rows == k, rrow, r)
        rt = jnp.where(cols == k, rcol, rt)
        a = a - rcol * rrow
        pivots.append(piv)
    x = jnp.zeros((n, n), jnp.float32)
    for i in range(n - 1, -1, -1):
        ident = jnp.where(lane == i, 1.0, 0.0)
        if i < n - 1:
            c = jnp.sum(jnp.where(cols == i, rt, 0.0), axis=1, keepdims=True)
            s = jnp.sum(jnp.where(sub > i, c * x, 0.0), axis=0, keepdims=True)
            ident = ident - s
        x = jnp.where(rows == i, ident / pivots[i], x)
    r_ref[...] = r
    x_ref[...] = x


def gram_kernel(sizes, count, g_ref, r_ref, x_ref, bx, by, bz, s1, s2, send_sem, recv_sem):
    bufs = (bx, by, bz)
    me = tuple(lax.axis_index(a) for a in AXES)

    def device(axis, index):
        return tuple(index if j == axis else me[j] for j in range(3))

    for buf in bufs:
        buf[...] = jnp.zeros_like(buf)
    barrier = pltpu.get_barrier_semaphore()
    peers = 0
    for axis in range(3):
        n = sizes[axis]
        for d in range(1, n):
            pl.semaphore_signal(barrier, inc=1, device_id=device(axis, (me[axis] + d) % n), device_id_type=pl.DeviceIdType.MESH)
            peers += 1
    pl.semaphore_wait(barrier, peers)

    src = g_ref
    total = None
    for axis, dst in zip(range(3), (s1, s2, None)):
        n = sizes[axis]
        m = me[axis]
        buf = bufs[axis]
        sends = []
        for d in range(1, n):
            copy = pltpu.make_async_remote_copy(
                src_ref=src,
                dst_ref=buf.at[m],
                send_sem=send_sem.at[axis, d],
                recv_sem=recv_sem.at[axis, m],
                device_id=device(axis, (m + d) % n),
                device_id_type=pl.DeviceIdType.MESH,
            )
            copy.start()
            sends.append(copy)
        for d in range(1, n):
            q = (m + n - d) % n
            pltpu.make_async_remote_copy(
                src_ref=src,
                dst_ref=buf.at[q],
                send_sem=send_sem.at[axis, d],
                recv_sem=recv_sem.at[axis, q],
                device_id=device(axis, q),
                device_id_type=pl.DeviceIdType.MESH,
            ).wait_recv()
        own = src[...]
        total = None
        for slot in range(n):
            value = jnp.where(m == slot, own, buf[slot])
            total = value if total is None else total + value
        for copy in sends:
            copy.wait_send()
        if dst is not None:
            dst[...] = total
            src = dst
    cholesky_and_inverse(total / count, r_ref, x_ref)


def factor_and_inverse(partial, count):
    n = partial.shape[0]
    sizes = tuple(lax.axis_size(a) for a in AXES)
    most = max(sizes)
    return pl.pallas_call(
        functools.partial(gram_kernel, sizes, count),
        out_shape=(
            jax.ShapeDtypeStruct((n, n), jnp.float32),
            jax.ShapeDtypeStruct((n, n), jnp.float32),
        ),
        scratch_shapes=[
            pltpu.VMEM((sizes[0], n, n), jnp.float32),
            pltpu.VMEM((sizes[1], n, n), jnp.float32),
            pltpu.VMEM((sizes[2], n, n), jnp.float32),
            pltpu.VMEM((n, n), jnp.float32),
            pltpu.VMEM((n, n), jnp.float32),
            pltpu.SemaphoreType.DMA((3, most)),
            pltpu.SemaphoreType.DMA((3, most)),
        ],
        compiler_params=pltpu.CompilerParams(collective_id=0, has_side_effects=True),
    )(partial)


def orthonormalize(rows, count):
    partial = jnp.dot(rows, rows.T, precision=lax.Precision.HIGHEST)
    factor, inverse = factor_and_inverse(partial, count)
    return (jnp.dot(inverse.T, rows, precision=lax.Precision.HIGHEST), factor)


def body(rhs, coef_x, coef_y, coef_z, diag_term):
    coefs = (coef_x, coef_y, coef_z)
    faces = []
    for axis, dim in enumerate((2, 3, 1)):
        last_f, first_f = end_faces(rhs, dim)
        last_c, first_c = end_faces(coefs[axis], dim - 1)
        faces.append((jnp.concatenate([last_f, last_c[None]], 0), jnp.concatenate([first_f, first_c[None]], 0)))
    got = exchange(faces, 1)
    lead = rhs.shape[0]
    (bx, ax), (by, ay), (bz, az) = [(b[:lead], a[:lead]) for b, a in got]
    up_x, lo_x = face_coefs(coef_x, 1, got[0][0][lead], got[0][1][lead])
    up_y, lo_y = face_coefs(coef_y, 2, got[1][0][lead], got[1][1][lead])
    up_z, lo_z = face_coefs(coef_z, 0, got[2][0][lead], got[2][1][lead])
    blocks = [rhs]
    field = rhs
    for section in range(STEPS):
        if section > 0:
            (bx, ax), (by, ay), (bz, az) = exchange([end_faces(field, d) for d in (2, 3, 1)], 2)
        mz, pz = shifted(field, 1, bz, az)
        mx, px = shifted(field, 2, bx, ax)
        my, py = shifted(field, 3, by, ay)
        center = field
        image = diag_term * center
        image = image + (up_z * (center - pz) + lo_z * (center - mz))
        image = image + (up_x * (center - px) + lo_x * (center - mx))
        image = image + (up_y * (center - py) + lo_y * (center - my))
        field = (image - NEWTON_SHIFTS[section] * field) * BASIS_SCALE
        blocks.append(field)
    basis = jnp.concatenate(blocks, 0)
    rows = basis.reshape(basis.shape[0], -1)
    count = float(rows.shape[1] * lax.axis_size("gx") * lax.axis_size("gy") * lax.axis_size("gz"))
    first, factor_one = orthonormalize(rows, count)
    second, factor_two = orthonormalize(first, count)
    return (
        second.reshape(basis.shape),
        jnp.dot(factor_two, factor_one, precision=lax.Precision.HIGHEST),
    )


def solution(mesh):
    return jax.shard_map(
        body,
        mesh=mesh,
        in_specs=(
            P(None, "gz", "gx", "gy"),
            P("gz", "gx", "gy"),
            P("gz", "gx", "gy"),
            P("gz", "gx", "gy"),
            P("gz", "gx", "gy"),
        ),
        out_specs=(P(None, "gz", "gx", "gy"), P()),
        check_vma=False,
    )
```
